32 devices in a mesh: groups: 2 (over y), shard: 4 (over z), section: 2 (over x), halo: 2 (over core).
Axes of the slice: x: 2, y: 2, z: 4, core: 2. Of those that a mesh axis runs over, the one named last changes fastest.
Arguments:
- features: bfloat16 [4, 4, 16, 64, 320], P(('groups', 'section'), 'shard', 'halo'), parts along dimension 0, may hold values from -6 to 6
- timesteps: int32 [4, 2], P(('groups', 'section')), parts along dimension 0, may hold values from 0 to 999
- conv_first: bfloat16 [2, 3, 3, 320, 320], P('section'), may hold values from -0.109375 to 0.109375
- conv_second: bfloat16 [2, 3, 3, 320, 320], P('section'), may hold values from -0.109375 to 0.109375
- time_weight: bfloat16 [2, 320, 320], P('section'), may hold values from -0.3125 to 0.3125
- qkv_weight: bfloat16 [2, 320, 960], P('section'), may hold values from -7 to 7
- attn_out: bfloat16 [2, 320, 320], P('section'), may hold values from -0.3125 to 0.3125
- geglu_in: bfloat16 [2, 320, 2560], P('section'), may hold values from -0.3125 to 0.3125
- geglu_out: bfloat16 [2, 1280, 320], P('section'), may hold values from -0.15625 to 0.15625
Outputs:
- result: bfloat16 [4, 4, 16, 64, 320], P(('groups', 'section'), 'shard', 'halo'), parts along dimension 0
The draws below stay inside these ranges and needn't reach their ends.
There are 2 independent parts, one for each index of `groups`. The reference program is written for one: setup_inputs(seed, part) draws one part's arguments, and reference() takes and returns one part's arrays. A program takes and returns all parts, laid end to end along the dimension named above; an argument that names none is the same for every part. Nothing has to cross between parts.
All inputs are finite; a program needn't handle non-finite values.
Results may differ from the reference program's by a relative error of at most 0.02.
Values may be sent and summed in bfloat16 or wider, within the bound.
A program may use at most 64 MiB of HBM per device.

```python
import math
import jax
import jax.numpy as jnp
from jax import lax

C = 320
HEAD_DIM = 64
FF = 1280
GROUPS = 32
WIDTH = 64
STEPS = 2
SECTIONS = 2
FRAMES = 4
HEIGHT = 16


def draw_qkv_weight(key, part):
    first_key, second_key, third_key = jax.random.split(jax.random.fold_in(key, 7), 3)
    scaling = C ** (-0.5)
    key_weight = jax.random.truncated_normal(second_key, -4.0, 4.0, (SECTIONS, C, C), jnp.float32) * scaling
    value_weight = jax.random.truncated_normal(third_key, -4.0, 4.0, (SECTIONS, C, C), jnp.float32) * scaling
    noise_weight = jax.random.truncated_normal(first_key, -4.0, 4.0, (SECTIONS, C, C), jnp.float32) * scaling
    query_weight = noise_weight
    return jnp.concatenate([query_weight, key_weight, value_weight], axis=2).astype(jnp.bfloat16)


def set_ends(drawn, own_key, low, largest):
    extent = drawn.shape
    spot = [jax.random.randint(jax.random.fold_in(own_key, axis), (), 0, extent[axis]) for axis in range(len(extent))]
    drawn = drawn.at[tuple(spot)].set(low)
    longest = extent.index(max(extent))
    spot[longest] = (spot[longest] + 1) % extent[longest]
    return drawn.at[tuple(spot)].set(largest)


def level_of(stream_key, dims, cuts, low, top_value):
    def one(axis_at, parts):
        steps = jax.random.uniform(jax.random.fold_in(jax.random.fold_in(stream_key, 6), axis_at), (parts,), jnp.float32, low / len(cuts), top_value / len(cuts))
        return jnp.repeat(jnp.exp(steps), dims[axis_at] // parts).reshape((-1,) + (1,) * (len(dims) - axis_at - 1))

    loudness = one(*cuts[0])
    for cut in cuts[1:]:
        loudness = loudness * one(*cut)
    return loudness


def gaussian(own_key, shape, scale, bound, pieces=(), kind=jnp.bfloat16):
    factor_of = level_of(own_key, shape, pieces, -0.22, 0.18) if pieces else 1.0
    result = jax.random.normal(own_key, shape, jnp.float32) * scale * factor_of
    return jnp.minimum(jnp.maximum(result, -bound), bound).astype(kind)


def setup_inputs(seed: int = 0, part: int = 0) -> dict:
    splits = jax.random.split(jax.random.key(seed), 10)
    part_keys = jax.random.split(jax.random.fold_in(splits[9], part), 10)
    return {
        "features": gaussian(part_keys[0], (SECTIONS, FRAMES, HEIGHT, WIDTH, C), 1.0, 6.0, ((0, 2), (1, 4), (2, 2))),
        "timesteps": set_ends(jax.random.randint(part_keys[1], (SECTIONS, STEPS), 0, 1000), jax.random.fold_in(part_keys[1], 1), 0, 999).astype(jnp.int32),
        "conv_first": gaussian(splits[2], (SECTIONS, 3, 3, C, C), (9 * C) ** -0.5, 0.109375, ((0, 2),)),
        "conv_second": gaussian(splits[3], (SECTIONS, 3, 3, C, C), (9 * C) ** -0.5, 0.109375, ((0, 2),)),
        "time_weight": gaussian(splits[4], (SECTIONS, C, C), C ** -0.5, 0.3125, ((0, 2),)),
        "qkv_weight": draw_qkv_weight(jax.random.fold_in(splits[9], 71), part),
        "attn_out": gaussian(splits[6], (SECTIONS, C, C), C ** -0.5, 0.3125, ((0, 2),)),
        "geglu_in": gaussian(splits[7], (SECTIONS, C, 2 * FF), C ** -0.5, 0.3125, ((0, 2),)),
        "geglu_out": gaussian(splits[8], (SECTIONS, FF, C), FF ** -0.5, 0.15625, ((0, 2),)),
    }


def norm_silu(field):
    frames, height, column_count, channels = field.shape
    grouped = field.reshape(frames, height * column_count, GROUPS, channels // GROUPS)
    average = lax.optimization_barrier(jnp.mean(grouped, axis=(1, 3), keepdims=True))
    squares = lax.optimization_barrier(jnp.mean(grouped * grouped, axis=(1, 3), keepdims=True))
    normed = (grouped - average) * lax.rsqrt(squares - average * average + 1e-05)
    return jax.nn.silu(normed).reshape(field.shape).astype(jnp.bfloat16)

def conv_frames(active, kernel):
    frames, height, column_count, channels = active.shape
    padded = jnp.pad(active, ((0, 0), (1, 1), (1, 1), (0, 0)))
    outcome = jnp.zeros((frames * height * column_count, kernel.shape[3]), jnp.float32)
    for row_offset in range(3):
        for column_offset in range(3):
            window = padded[:, row_offset:row_offset + height, column_offset:column_offset + column_count, :]
            outcome = outcome + jnp.dot(window.reshape(-1, channels), kernel[row_offset, column_offset], preferred_element_type=jnp.float32)
    return outcome.reshape(frames, height, column_count, kernel.shape[3])

def embed_time(stamp, time_weight):
    half_width = time_weight.shape[0] // 2
    frequency = jnp.exp(-math.log(10000.0) * jnp.arange(half_width, dtype=jnp.float32) / half_width)
    angles = stamp.astype(jnp.float32) * frequency
    sinusoid = jnp.concatenate([jnp.cos(angles), jnp.sin(angles)])
    return jnp.dot(jax.nn.silu(sinusoid).astype(jnp.bfloat16)[None, :], time_weight, preferred_element_type=jnp.float32)[0]

def layer_norm(stream):
    values_f = stream.astype(jnp.float32)
    average = lax.optimization_barrier(jnp.mean(values_f, axis=-1, keepdims=True))
    centred = values_f - average
    spread = lax.optimization_barrier(jnp.mean(centred * centred, axis=-1, keepdims=True))
    return (centred * lax.rsqrt(spread + 1e-05)).astype(jnp.bfloat16)

def attend(query, key_block, value_block):
    query_frames, pixels, channels = query.shape
    head_count = channels // HEAD_DIM

    def split_heads(tensor):
        return tensor.reshape(tensor.shape[0], tensor.shape[1], head_count, HEAD_DIM).astype(jnp.float32)
    scores = jnp.einsum('fphd,gphd->phfg', split_heads(query), split_heads(key_block)) * HEAD_DIM ** (-0.5)
    weights = jax.nn.softmax(scores, axis=-1).astype(jnp.bfloat16)
    mixed = jnp.einsum('phfg,gphd->fphd', weights.astype(jnp.float32), split_heads(value_block))
    return mixed.reshape(query_frames, pixels, channels).astype(jnp.bfloat16)

def temporal(stream, qkv_weight, attn_out):
    frames, pixels, channels = stream.shape
    normed = layer_norm(stream).reshape(-1, channels)
    projected = jnp.dot(normed, qkv_weight, preferred_element_type=jnp.float32).astype(jnp.bfloat16)
    projected = projected.reshape(frames, pixels, 3 * channels)
    mixed = attend(projected[:, :, :channels], projected[:, :, channels:2 * channels], projected[:, :, 2 * channels:])
    update = jnp.dot(mixed.reshape(-1, channels), attn_out, preferred_element_type=jnp.float32).reshape(stream.shape)
    return (stream.astype(jnp.float32) + update).astype(jnp.bfloat16)

def feed(stream, geglu_in, geglu_out):
    channels = stream.shape[2]
    inner = geglu_out.shape[0]
    normed = layer_norm(stream).reshape(-1, channels)
    projected = jnp.dot(normed, geglu_in, preferred_element_type=jnp.float32)
    active = (projected[:, :inner] * jax.nn.gelu(projected[:, inner:], approximate=False)).astype(jnp.bfloat16)
    update = jnp.dot(active, geglu_out, preferred_element_type=jnp.float32).reshape(stream.shape)
    return (stream.astype(jnp.float32) + update).astype(jnp.bfloat16)

def section_block(field, stamp, conv_first, conv_second, time_weight, qkv_weight, attn_out, geglu_in, geglu_out):
    frames, height, column_count, channels = field.shape
    base = field.astype(jnp.float32)
    first = conv_frames(norm_silu(base), conv_first) + embed_time(stamp, time_weight)
    second = conv_frames(norm_silu(first), conv_second)
    stream = (base + second).astype(jnp.bfloat16).reshape(frames, height * column_count, channels)
    stream = temporal(stream, qkv_weight, attn_out)
    stream = feed(stream, geglu_in, geglu_out)
    return stream.reshape(field.shape)

def reference(features, timesteps, conv_first, conv_second, time_weight, qkv_weight, attn_out, geglu_in, geglu_out):
    current = features
    for denoise_step in range(STEPS):
        current = jnp.roll(current, 1, axis=0)
        outputs = []
        for section in range(SECTIONS):
            outputs.append(section_block(current[section], timesteps[section, denoise_step], conv_first[section], conv_second[section], time_weight[section], qkv_weight[section], attn_out[section], geglu_in[section], geglu_out[section]))
        current = jnp.stack(outputs)
    return current
```

```python
import functools
import math

import jax
import jax.numpy as jnp
from jax import lax
from jax.experimental import pallas as pl
from jax.experimental.pallas import tpu as pltpu
from jax.sharding import PartitionSpec as P

HEAD_DIM = 64
GROUPS = 32
STEPS = 2
MESH = pl.DeviceIdType.MESH
F32 = jnp.float32
BF16 = jnp.bfloat16
BLK = 64
PAD = 8


def matmul(a, b):
    return jnp.dot(a, b, preferred_element_type=F32)


def silu(u):
    return u * (1.0 / (1.0 + jnp.exp(-u)))


def kernel(dims, stamps, feat, cf_h, cs_h, tw_h, qkv_h, ao_h, gi_h, go_h, out, *scratch):
    (rows, width, chans, inner, nsh, nsec) = dims
    (F, H, G, A, S, PB, O, stat_tx, stat_rx, edge_x, edge_h, emb, gmask, hmask, hmask_t,
     N, Q, K, V, PH, PL, OB, S2, ACT,
     cf, cs, tw, qkv, ao, gi, go,
     w_sem, x_sem, halo_send, halo_recv, in_send, in_recv, out_send, out_recv, own_sem) = scratch
    tokens = rows * width
    part = tokens // nsh
    rim = (rows + 2) * width
    me = lax.axis_index("shard")
    sec = lax.axis_index("section")
    side = lax.axis_index("halo")
    nxt = lax.rem(sec + 1, nsec)

    loads = [
        pltpu.make_async_copy(src, dst, w_sem.at[i])
        for i, (src, dst) in enumerate(
            ((cf_h, cf), (cs_h, cs), (tw_h, tw), (qkv_h, qkv), (ao_h, ao), (gi_h, gi), (go_h, go))
        )
    ]
    for load in loads:
        load.start()

    def at(shard, section):
        return {"shard": shard, "section": section}

    barrier = pltpu.get_barrier_semaphore()
    peers = [{"halo": 1 - side}]
    for d in range(1, nsh):
        peers.append(at(lax.rem(me + d, nsh), sec))
    for e in sorted({1 % nsec, (nsec - 1) % nsec} - {0}):
        for d in range(nsh):
            peers.append(at(lax.rem(me + d, nsh), lax.rem(sec + e, nsec)))
    for peer in peers:
        pl.semaphore_signal(barrier, inc=1, device_id=peer, device_id_type=MESH)
    pl.semaphore_wait(barrier, len(peers))

    shift = pltpu.make_async_remote_copy(
        src_ref=feat, dst_ref=F.at[0], send_sem=x_sem.at[0], recv_sem=x_sem.at[1],
        device_id={"section": nxt}, device_id_type=MESH,
    )
    shift.start()

    per = chans // GROUPS
    ci = lax.broadcasted_iota(jnp.int32, (chans, chans), 0)
    cj = lax.broadcasted_iota(jnp.int32, (chans, chans), 1)
    gmask[...] = jnp.where(ci - lax.rem(ci, per) == cj - lax.rem(cj, per), 1.0, 0.0).astype(F32)
    lanes = hmask.shape[1]
    hi_ = lax.broadcasted_iota(jnp.int32, (chans, lanes), 0)
    hj_ = lax.broadcasted_iota(jnp.int32, (chans, lanes), 1)
    hmask[...] = jnp.where(hi_ - lax.rem(hi_, HEAD_DIM) == hj_ * HEAD_DIM, HEAD_DIM ** (-0.5), 0.0).astype(BF16)
    ti_ = lax.broadcasted_iota(jnp.int32, (lanes, chans), 0)
    tj_ = lax.broadcasted_iota(jnp.int32, (lanes, chans), 1)
    hmask_t[...] = jnp.where(tj_ - lax.rem(tj_, HEAD_DIM) == ti_ * HEAD_DIM, 1.0, 0.0).astype(BF16)
    stat_tx[...] = jnp.zeros_like(stat_tx)
    zeros_rim = jnp.zeros((width, chans), F32)
    G[pl.ds(0, PAD), :] = jnp.zeros((PAD, chans), F32)
    G[pl.ds(PAD + rim, PAD), :] = jnp.zeros((PAD, chans), F32)
    G[pl.ds(PAD, width), :] = zeros_rim
    G[pl.ds(PAD + rim - width, width), :] = zeros_rim

    loads[2].wait()
    half = chans // 2
    lane = lax.broadcasted_iota(jnp.int32, (16, chans), 1)
    k_of = jnp.where(lane < half, lane, lane - half).astype(F32)
    frequency = jnp.exp(-math.log(10000.0) * k_of / half)
    for n in range(STEPS):
        angles = stamps[0, n].astype(F32) * frequency
        wave = jnp.where(lane < half, jnp.cos(angles), jnp.sin(angles))
        emb[n] = matmul(silu(wave).astype(BF16), tw[...])

    edge_at = pl.multiple_of((1 - side) * (tokens - width), 16)
    rim_at = pl.multiple_of(PAD + (1 - side) * (rim - width), 8)
    count = float(rows * 2 * width * per)

    def swap(slot, edge_src, edge_dst):
        copies = [
            pltpu.make_async_remote_copy(
                src_ref=src, dst_ref=dst, send_sem=halo_send.at[slot, i], recv_sem=halo_recv.at[slot, i],
                device_id={"halo": 1 - side}, device_id_type=MESH,
            )
            for i, (src, dst) in enumerate(
                ((edge_src, edge_dst), (stat_tx.at[slot], stat_rx.at[slot]))
            )
        ]
        return copies

    def totals(load, slot):
        def one(i, carry):
            s1, s2 = carry
            v = load(pl.ds(pl.multiple_of(i * BLK, BLK), BLK))
            return (s1 + jnp.sum(v.reshape(BLK // 8, 8, chans), axis=0),
                    s2 + jnp.sum((v * v).reshape(BLK // 8, 8, chans), axis=0))
        z = jnp.zeros((8, chans), F32)
        s1, s2 = lax.fori_loop(0, tokens // BLK, one, (z, z))
        stat_tx[slot, 0:1, :] = jnp.sum(s1, axis=0, keepdims=True)
        stat_tx[slot, 1:2, :] = jnp.sum(s2, axis=0, keepdims=True)

    def moments(slot):
        both = stat_tx[slot] + stat_rx[slot]
        summed = jnp.dot(both, gmask[...], preferred_element_type=F32, precision=lax.Precision.HIGHEST)
        average = summed[0:1, :] / count
        second = summed[1:2, :] / count
        return average, lax.rsqrt(second - average * average + 1e-05)

    def activate(load, load_edge, slot):
        average, inverse = moments(slot)

        def one(i, c):
            at_ = pl.multiple_of(i * BLK, BLK)
            G[pl.ds(PAD + width + at_, BLK), :] = silu((load(pl.ds(at_, BLK)) - average) * inverse)
            return c
        lax.fori_loop(0, tokens // BLK, one, 0)
        G[pl.ds(rim_at, width), :] = silu((load_edge() - average) * inverse)
        col = lax.rem(lax.broadcasted_iota(jnp.int32, (width, chans), 0), width)

        def two(i, c):
            at_ = pl.multiple_of(i * width, width)
            window = G[pl.ds(at_, width + 2 * PAD), :]
            left = window[PAD - 1 : PAD - 1 + width]
            mid = window[PAD : PAD + width]
            right = window[PAD + 1 : PAD + 1 + width]
            dst = pl.ds(at_, width)
            A[dst, 0:chans] = jnp.where(col == 0, 0.0, left).astype(BF16)
            A[dst, chans : 2 * chans] = mid.astype(BF16)
            A[dst, 2 * chans :] = jnp.where(col == width - 1, 0.0, right).astype(BF16)
            return c
        lax.fori_loop(0, rows + 2, two, 0)

    def conv(weights):
        total = matmul(A[pl.ds(0, tokens), :], weights[0])
        total += matmul(A[pl.ds(width, tokens), :], weights[1])
        total += matmul(A[pl.ds(2 * width, tokens), :], weights[2])
        return total

    def normalise(src):
        def one(i, c):
            at_ = pl.ds(pl.multiple_of(i * BLK, BLK), BLK)
            v = src(at_)
            centred = v - jnp.mean(v, axis=-1, keepdims=True)
            spread = jnp.mean(centred * centred, axis=-1, keepdims=True)
            N[at_, :] = (centred * lax.rsqrt(spread + 1e-05)).astype(BF16)
            return c
        lax.fori_loop(0, tokens // BLK, one, 0)

    for n in range(STEPS):
        if n == 0:
            shift.wait()
        field = F.at[n]

        def load_x(s, field=field):
            return field[s, :].astype(F32)

        swaps = swap(2 * n, field.at[pl.ds(edge_at, width)], edge_x.at[n])
        swaps[0].start()
        totals(load_x, 2 * n)
        swaps[1].start()
        for s in swaps:
            s.wait()
        activate(load_x, lambda: edge_x[n].astype(F32), 2 * n)
        if n == 0:
            loads[0].wait()
        H[n] = conv(cf) + emb[n, 0:1, :]

        def load_h(s):
            return H[n, s, :]
        swaps = swap(2 * n + 1, H.at[n, pl.ds(edge_at, width)], edge_h.at[n])
        swaps[0].start()
        totals(load_h, 2 * n + 1)
        swaps[1].start()
        for s in swaps:
            s.wait()
        activate(load_h, lambda: edge_h[n], 2 * n + 1)
        if n == 0:
            loads[1].wait()
        S[n] = (conv(cs) + field[...].astype(F32)).astype(BF16).reshape(nsh, part, chans)

        copies = []
        for d in range(1, nsh):
            to = lax.rem(me + d, nsh)
            copies.append(pltpu.make_async_remote_copy(
                src_ref=S.at[n, to], dst_ref=PB.at[n, me],
                send_sem=in_send.at[n, d], recv_sem=in_recv.at[n, d],
                device_id={"shard": to}, device_id_type=MESH,
            ))
            copies[-1].start()
        PB[n, me] = S[n, me]
        for c in copies:
            c.wait()

        if n == 0:
            for i in (3, 4, 5, 6):
                loads[i].wait()
        stream = PB.at[n]

        def load_p(s):
            return stream.reshape(tokens, chans)[s, :].astype(F32)
        normalise(load_p)
        proj = matmul(N[...], qkv[...]).astype(BF16)
        Q[...] = proj[:, :chans].astype(F32)
        K[...] = proj[:, chans : 2 * chans].astype(F32)
        V[...] = proj[:, 2 * chans :].astype(F32)

        def frame(f, c):
            q = Q[pl.ds(pl.multiple_of(f * part, 16), part), :]
            for g in range(nsh):
                prod = q * K[g * part : (g + 1) * part, :]
                high = prod.astype(BF16)
                PH[g * part : (g + 1) * part, :] = high
                PL[g * part : (g + 1) * part, :] = (prod - high.astype(F32)).astype(BF16)
            score = matmul(PH[...], hmask[...]) + matmul(PL[...], hmask[...])
            pieces = [score[g * part : (g + 1) * part] for g in range(nsh)]
            top = functools.reduce(jnp.maximum, pieces)
            pieces = [jnp.exp(p - top) for p in pieces]
            scale = 1.0 / functools.reduce(jnp.add, pieces)
            mixed = jnp.zeros((part, chans), F32)
            for g in range(nsh):
                weight = matmul((pieces[g] * scale).astype(BF16), hmask_t[...])
                mixed = mixed + weight * V[g * part : (g + 1) * part, :]
            OB[pl.ds(pl.multiple_of(f * part, 16), part), :] = mixed.astype(BF16)
            return c
        lax.fori_loop(0, nsh, frame, 0)

        S2[...] = (matmul(OB[...], ao[...]) + stream[...].reshape(tokens, chans).astype(F32)).astype(BF16)
        normalise(lambda s: S2[s, :].astype(F32))
        wide = 256
        for j in range(inner // wide):
            value = matmul(N[...], gi[:, j * wide : (j + 1) * wide])
            gate = matmul(N[...], gi[:, inner + j * wide : inner + (j + 1) * wide])
            gelu = 0.5 * gate * (1.0 + lax.erf(gate * (0.5 ** 0.5)))
            ACT[:, j * wide : (j + 1) * wide] = (value * gelu).astype(BF16)
        O[n] = (matmul(ACT[...], go[...]) + S2[...].astype(F32)).astype(BF16).reshape(nsh, part, chans)

        last = n == STEPS - 1
        landing = pl.ds(pl.multiple_of(me * part, 16), part)
        target = out if last else F.at[n + 1]
        copies = []
        for d in range(nsh):
            to = lax.rem(me + d, nsh)
            if d == 0 and (last or nsec == 1):
                copies.append(pltpu.make_async_copy(O.at[n, me], target.at[landing], own_sem.at[n]))
            else:
                copies.append(pltpu.make_async_remote_copy(
                    src_ref=O.at[n, to], dst_ref=target.at[landing],
                    send_sem=out_send.at[n, d], recv_sem=out_recv.at[n, d],
                    device_id=at(to, sec if last else nxt), device_id_type=MESH,
                ))
            copies[-1].start()
        for c in copies:
            c.wait()


def solution(mesh):
    nsh, nsec = mesh.shape["shard"], mesh.shape["section"]

    def per_device(features, timesteps, conv_first, conv_second, time_weight, qkv_weight,
                   attn_out, geglu_in, geglu_out):
        _, _, rows, width, chans = features.shape
        inner = geglu_out.shape[1]
        tokens = rows * width
        part = tokens // nsh
        rim = (rows + 2) * width
        dims = (rows, width, chans, inner, nsh, nsec)
        any_ = pl.BlockSpec(memory_space=pl.ANY)
        V = pltpu.VMEM
        D = pltpu.SemaphoreType.DMA
        scratch = [
            V((STEPS, tokens, chans), BF16),
            V((STEPS, tokens, chans), F32),
            V((rim + 2 * PAD, chans), F32),
            V((rim, 3 * chans), BF16),
            V((STEPS, nsh, part, chans), BF16),
            V((STEPS, nsh, part, chans), BF16),
            V((STEPS, nsh, part, chans), BF16),
            V((2 * STEPS, 8, chans), F32),
            V((2 * STEPS, 8, chans), F32),
            V((STEPS, width, chans), BF16),
            V((STEPS, width, chans), F32),
            V((STEPS, 16, chans), F32),
            V((chans, chans), F32),
            V((chans, 128), BF16),
            V((128, chans), BF16),
            V((tokens, chans), BF16),
            V((tokens, chans), F32), V((tokens, chans), F32), V((tokens, chans), F32),
            V((tokens, chans), BF16), V((tokens, chans), BF16),
            V((tokens, chans), BF16), V((tokens, chans), BF16), V((tokens, inner), BF16),
            V((3, 3 * chans, chans), BF16), V((3, 3 * chans, chans), BF16),
            V((chans, chans), BF16), V((chans, 3 * chans), BF16), V((chans, chans), BF16),
            V((chans, 2 * inner), BF16), V((inner, chans), BF16),
            D((7,)), D((2,)), D((2 * STEPS, 2)), D((2 * STEPS, 2)),
            D((STEPS, nsh)), D((STEPS, nsh)), D((STEPS, nsh)), D((STEPS, nsh)), D((STEPS,)),
        ]
        result = pl.pallas_call(
            functools.partial(kernel, dims),
            out_shape=jax.ShapeDtypeStruct((tokens, chans), BF16),
            in_specs=[pl.BlockSpec(memory_space=pltpu.SMEM)] + [any_] * 8,
            out_specs=any_,
            scratch_shapes=scratch,
            compiler_params=pltpu.CompilerParams(
                collective_id=0, has_side_effects=True, vmem_limit_bytes=60 * 1024 * 1024
            ),
        )(
            timesteps,
            features.reshape(tokens, chans),
            conv_first.reshape(3, 3 * chans, chans),
            conv_second.reshape(3, 3 * chans, chans),
            time_weight[0], qkv_weight[0], attn_out[0], geglu_in[0], geglu_out[0],
        )
        return result.reshape(features.shape)

    return jax.shard_map(
        per_device,
        mesh=mesh,
        in_specs=(
            P(("groups", "section"), "shard", "halo", None, None),
            P(("groups", "section"), None),
            P("section", None, None, None, None),
            P("section", None, None, None, None),
            P("section", None, None),
            P("section", None, None),
            P("section", None, None),
            P("section", None, None),
            P("section", None, None),
        ),
        out_specs=P(("groups", "section"), "shard", "halo", None, None),
        check_vma=False,
    )
```

```python
import functools
import math

import jax
import jax.numpy as jnp
from jax import lax
from jax.experimental import pallas as pl
from jax.experimental.pallas import tpu as pltpu
from jax.sharding import PartitionSpec as P

HEAD_DIM = 64
GROUPS = 32
STEPS = 2
MESH = pl.DeviceIdType.MESH
F32 = jnp.float32
BF16 = jnp.bfloat16
BLK = 64
SUBS = 2
UNROLL = 4
PAD = 8


def matmul(a, b):
    return jnp.dot(a, b, preferred_element_type=F32)


def silu(u):
    return u * (1.0 / (1.0 + jnp.exp(-u)))


def kernel(dims, stamps, feat, cf_h, cs_h, tw_h, qkv_h, ao_h, gi_h, go_h, out, *scratch):
    (rows, width, chans, inner, nsh, nsec, subs) = dims
    (F, H, G, A, S, PB, O, stat_tx, stat_rx, edge_x, edge_h, emb, gmask, hmask, hmask_t,
     N, Q, K, V, PH, PL, OB, S2, ACT,
     cf, cs, tw, qkv, ao, gi, go,
     w_sem, x_sem, halo_send, halo_recv, in_send, in_recv, out_send, out_recv, own_sem) = scratch
    tokens = rows * width
    part = tokens // nsh
    sub = part // subs
    crowd = nsh * sub
    rim = (rows + 2) * width
    me = lax.axis_index("shard")
    sec = lax.axis_index("section")
    side = lax.axis_index("halo")
    nxt = lax.rem(sec + 1, nsec)

    loads = [
        pltpu.make_async_copy(src, dst, w_sem.at[i])
        for i, (src, dst) in enumerate(
            ((cf_h, cf), (cs_h, cs), (tw_h, tw), (qkv_h, qkv), (ao_h, ao), (gi_h, gi), (go_h, go))
        )
    ]
    for load in loads:
        load.start()

    def at(shard, section):
        return {"shard": shard, "section": section}

    barrier = pltpu.get_barrier_semaphore()
    peers = [{"halo": 1 - side}]
    for d in range(1, nsh):
        peers.append(at(lax.rem(me + d, nsh), sec))
    for e in sorted({1 % nsec, (nsec - 1) % nsec} - {0}):
        for d in range(nsh):
            peers.append(at(lax.rem(me + d, nsh), lax.rem(sec + e, nsec)))
    for peer in peers:
        pl.semaphore_signal(barrier, inc=1, device_id=peer, device_id_type=MESH)
    pl.semaphore_wait(barrier, len(peers))

    shift = pltpu.make_async_remote_copy(
        src_ref=feat, dst_ref=F.at[0], send_sem=x_sem.at[0], recv_sem=x_sem.at[1],
        device_id={"section": nxt}, device_id_type=MESH,
    )
    shift.start()

    per = chans // GROUPS
    ci = lax.broadcasted_iota(jnp.int32, (chans, chans), 0)
    cj = lax.broadcasted_iota(jnp.int32, (chans, chans), 1)
    gmask[...] = jnp.where(ci - lax.rem(ci, per) == cj - lax.rem(cj, per), 1.0, 0.0).astype(F32)
    lanes = hmask.shape[1]
    hi_ = lax.broadcasted_iota(jnp.int32, (chans, lanes), 0)
    hj_ = lax.broadcasted_iota(jnp.int32, (chans, lanes), 1)
    hmask[...] = jnp.where(hi_ - lax.rem(hi_, HEAD_DIM) == hj_ * HEAD_DIM, HEAD_DIM ** (-0.5), 0.0).astype(BF16)
    ti_ = lax.broadcasted_iota(jnp.int32, (lanes, chans), 0)
    tj_ = lax.broadcasted_iota(jnp.int32, (lanes, chans), 1)
    hmask_t[...] = jnp.where(tj_ - lax.rem(tj_, HEAD_DIM) == ti_ * HEAD_DIM, 1.0, 0.0).astype(BF16)
    stat_tx[...] = jnp.zeros_like(stat_tx)
    zeros_rim = jnp.zeros((width, chans), F32)
    G[pl.ds(0, PAD), :] = jnp.zeros((PAD, chans), F32)
    G[pl.ds(PAD + rim, PAD), :] = jnp.zeros((PAD, chans), F32)
    G[pl.ds(PAD, width), :] = zeros_rim
    G[pl.ds(PAD + rim - width, width), :] = zeros_rim

    loads[2].wait()
    half = chans // 2
    lane = lax.broadcasted_iota(jnp.int32, (16, chans), 1)
    k_of = jnp.where(lane < half, lane, lane - half).astype(F32)
    frequency = jnp.exp(-math.log(10000.0) * k_of / half)
    for n in range(STEPS):
        angles = stamps[0, n].astype(F32) * frequency
        wave = jnp.where(lane < half, jnp.cos(angles), jnp.sin(angles))
        emb[n] = matmul(silu(wave).astype(BF16), tw[...])

    edge_at = pl.multiple_of((1 - side) * (tokens - width), 16)
    rim_at = pl.multiple_of(PAD + (1 - side) * (rim - width), 8)
    count = float(rows * 2 * width * per)

    def swap(slot, edge_src, edge_dst):
        copies = [
            pltpu.make_async_remote_copy(
                src_ref=src, dst_ref=dst, send_sem=halo_send.at[slot, i], recv_sem=halo_recv.at[slot, i],
                device_id={"halo": 1 - side}, device_id_type=MESH,
            )
            for i, (src, dst) in enumerate(
                ((edge_src, edge_dst), (stat_tx.at[slot], stat_rx.at[slot]))
            )
        ]
        return copies

    def totals(load, slot):
        def one(i, carry):
            s1, s2 = carry
            v = load(pl.ds(pl.multiple_of(i * BLK, BLK), BLK))
            return (s1 + jnp.sum(v.reshape(BLK // 8, 8, chans), axis=0),
                    s2 + jnp.sum((v * v).reshape(BLK // 8, 8, chans), axis=0))
        z = jnp.zeros((8, chans), F32)
        s1, s2 = lax.fori_loop(0, tokens // BLK, one, (z, z), unroll=UNROLL)
        stat_tx[slot, 0:1, :] = jnp.sum(s1, axis=0, keepdims=True)
        stat_tx[slot, 1:2, :] = jnp.sum(s2, axis=0, keepdims=True)

    def moments(slot):
        both = stat_tx[slot] + stat_rx[slot]
        summed = jnp.dot(both, gmask[...], preferred_element_type=F32, precision=lax.Precision.HIGHEST)
        average = summed[0:1, :] / count
        second = summed[1:2, :] / count
        return average, lax.rsqrt(second - average * average + 1e-05)

    def activate(load, load_edge, slot):
        average, inverse = moments(slot)

        def one(i, c):
            at_ = pl.multiple_of(i * BLK, BLK)
            G[pl.ds(PAD + width + at_, BLK), :] = silu((load(pl.ds(at_, BLK)) - average) * inverse)
            return c
        lax.fori_loop(0, tokens // BLK, one, 0, unroll=UNROLL)
        G[pl.ds(rim_at, width), :] = silu((load_edge() - average) * inverse)
        col = lax.rem(lax.broadcasted_iota(jnp.int32, (width, chans), 0), width)

        def two(i, c):
            at_ = pl.multiple_of(i * width, width)
            window = G[pl.ds(at_, width + 2 * PAD), :]
            left = window[PAD - 1 : PAD - 1 + width]
            mid = window[PAD : PAD + width]
            right = window[PAD + 1 : PAD + 1 + width]
            dst = pl.ds(at_, width)
            A[dst, 0:chans] = jnp.where(col == 0, 0.0, left).astype(BF16)
            A[dst, chans : 2 * chans] = mid.astype(BF16)
            A[dst, 2 * chans :] = jnp.where(col == width - 1, 0.0, right).astype(BF16)
            return c
        lax.fori_loop(0, rows + 2, two, 0, unroll=5)

    def conv(weights):
        total = matmul(A[pl.ds(0, tokens), :], weights[0])
        total += matmul(A[pl.ds(width, tokens), :], weights[1])
        total += matmul(A[pl.ds(2 * width, tokens), :], weights[2])
        return total

    def normalise(src):
        def one(i, c):
            at_ = pl.ds(pl.multiple_of(i * BLK, BLK), BLK)
            v = src(at_)
            centred = v - jnp.mean(v, axis=-1, keepdims=True)
            spread = jnp.mean(centred * centred, axis=-1, keepdims=True)
            N[at_, :] = (centred * lax.rsqrt(spread + 1e-05)).astype(BF16)
            return c
        lax.fori_loop(0, crowd // BLK, one, 0, unroll=UNROLL)

    def gather_copy(n, k, d):
        to = lax.rem(me + d, nsh)
        return pltpu.make_async_remote_copy(
            src_ref=S.at[n, k, to], dst_ref=PB.at[n, k, me],
            send_sem=in_send.at[n, k, d], recv_sem=in_recv.at[n, k, d],
            device_id={"shard": to}, device_id_type=MESH,
        )

    def return_copy(n, k, d):
        last = n == STEPS - 1
        target = out if last else F.at[n + 1]
        landing = target.at[pl.ds(pl.multiple_of(me * part + k * sub, 16), sub)]
        to = lax.rem(me + d, nsh)
        if d == 0 and (last or nsec == 1):
            return pltpu.make_async_copy(O.at[n, k, me], landing, own_sem.at[n, k])
        return pltpu.make_async_remote_copy(
            src_ref=O.at[n, k, to], dst_ref=landing,
            send_sem=out_send.at[n, k, d], recv_sem=out_recv.at[n, k, d],
            device_id=at(to, sec if last else nxt), device_id_type=MESH,
        )

    def pixels(n, k):
        stream = PB.at[n, k]

        def load_p(s):
            return stream.reshape(crowd, chans)[s, :].astype(F32)
        normalise(load_p)
        proj = matmul(N[...], qkv[...]).astype(BF16)
        Q[...] = proj[:, :chans].astype(F32)
        K[...] = proj[:, chans : 2 * chans].astype(F32)
        V[...] = proj[:, 2 * chans :].astype(F32)

        def frame(f, c):
            q = Q[pl.ds(pl.multiple_of(f * sub, 16), sub), :]
            start = pl.multiple_of(f * crowd, 16)
            for g in range(nsh):
                prod = q * K[g * sub : (g + 1) * sub, :]
                high = prod.astype(BF16)
                PH[pl.ds(start + g * sub, sub), :] = high
                PL[pl.ds(start + g * sub, sub), :] = (prod - high.astype(F32)).astype(BF16)
            score = matmul(PH[pl.ds(start, crowd), :], hmask[...]) + matmul(PL[pl.ds(start, crowd), :], hmask[...])
            pieces = [score[g * sub : (g + 1) * sub] for g in range(nsh)]
            top = functools.reduce(jnp.maximum, pieces)
            pieces = [jnp.exp(p - top) for p in pieces]
            scale = 1.0 / functools.reduce(jnp.add, pieces)
            weights = jnp.concatenate([(p * scale).astype(BF16) for p in pieces], axis=0)
            weights = matmul(weights, hmask_t[...])
            mixed = weights[0:sub] * V[0:sub, :]
            for g in range(1, nsh):
                mixed = mixed + weights[g * sub : (g + 1) * sub] * V[g * sub : (g + 1) * sub, :]
            OB[pl.ds(pl.multiple_of(f * sub, 16), sub), :] = mixed.astype(BF16)
            return c
        lax.fori_loop(0, nsh, frame, 0, unroll=4)

        S2[...] = (matmul(OB[...], ao[...]) + stream[...].reshape(crowd, chans).astype(F32)).astype(BF16)
        normalise(lambda s: S2[s, :].astype(F32))
        wide = 256
        for j in range(inner // wide):
            value = matmul(N[...], gi[:, j * wide : (j + 1) * wide])
            gate = matmul(N[...], gi[:, inner + j * wide : inner + (j + 1) * wide])
            gelu = 0.5 * gate * (1.0 + lax.erf(gate * (0.5 ** 0.5)))
            ACT[:, j * wide : (j + 1) * wide] = (value * gelu).astype(BF16)
        O[n, k] = (matmul(ACT[...], go[...]) + S2[...].astype(F32)).astype(BF16).reshape(nsh, sub, chans)

    for n in range(STEPS):
        if n == 0:
            shift.wait()
        field = F.at[n]

        def load_x(s, field=field):
            return field[s, :].astype(F32)

        swaps = swap(2 * n, field.at[pl.ds(edge_at, width)], edge_x.at[n])
        swaps[0].start()
        totals(load_x, 2 * n)
        swaps[1].start()
        for s in swaps:
            s.wait()
        activate(load_x, lambda: edge_x[n].astype(F32), 2 * n)
        if n == 0:
            loads[0].wait()
        H[n] = conv(cf) + emb[n, 0:1, :]

        def load_h(s):
            return H[n, s, :]
        swaps = swap(2 * n + 1, H.at[n, pl.ds(edge_at, width)], edge_h.at[n])
        swaps[0].start()
        totals(load_h, 2 * n + 1)
        swaps[1].start()
        for s in swaps:
            s.wait()
        activate(load_h, lambda: edge_h[n], 2 * n + 1)
        if n == 0:
            loads[1].wait()
        for k in range(subs):
            spans = [j * part + k * sub for j in range(nsh)]
            total = sum(
                matmul(jnp.concatenate([A[pl.ds(r * width + a, sub), :] for a in spans], axis=0), cs[r])
                for r in range(3)
            )
            base = jnp.concatenate([field[pl.ds(a, sub), :] for a in spans], axis=0)
            S[n, k] = (total + base.astype(F32)).astype(BF16).reshape(nsh, sub, chans)
            for d in range(1, nsh):
                gather_copy(n, k, d).start()
            PB[n, k, me] = S[n, k, me]

        if n == 0:
            for i in (3, 4, 5, 6):
                loads[i].wait()

        def temporal(k, carry, n=n):
            for d in range(1, nsh):
                gather_copy(n, k, d).wait_recv()
            pixels(n, k)
            for d in range(nsh):
                return_copy(n, k, d).start()
            return carry
        lax.fori_loop(0, subs, temporal, 0)

        def settle(k, carry, n=n):
            for d in range(1, nsh):
                gather_copy(n, k, d).wait_send()
            for d in range(nsh):
                return_copy(n, k, d).wait()
            return carry
        lax.fori_loop(0, subs, settle, 0)


def solution(mesh):
    nsh, nsec = mesh.shape["shard"], mesh.shape["section"]

    def per_device(features, timesteps, conv_first, conv_second, time_weight, qkv_weight,
                   attn_out, geglu_in, geglu_out):
        _, _, rows, width, chans = features.shape
        inner = geglu_out.shape[1]
        tokens = rows * width
        part = tokens // nsh
        rim = (rows + 2) * width
        subs = min(SUBS, part // 16)
        dims = (rows, width, chans, inner, nsh, nsec, subs)
        sub = part // subs
        crowd = nsh * sub
        any_ = pl.BlockSpec(memory_space=pl.ANY)
        V = pltpu.VMEM
        D = pltpu.SemaphoreType.DMA
        scratch = [
            V((STEPS, tokens, chans), BF16),
            V((STEPS, tokens, chans), F32),
            V((rim + 2 * PAD, chans), F32),
            V((rim, 3 * chans), BF16),
            V((STEPS, subs, nsh, sub, chans), BF16),
            V((STEPS, subs, nsh, sub, chans), BF16),
            V((STEPS, subs, nsh, sub, chans), BF16),
            V((2 * STEPS, 8, chans), F32),
            V((2 * STEPS, 8, chans), F32),
            V((STEPS, width, chans), BF16),
            V((STEPS, width, chans), F32),
            V((STEPS, 16, chans), F32),
            V((chans, chans), F32),
            V((chans, 128), BF16),
            V((128, chans), BF16),
            V((crowd, chans), BF16),
            V((crowd, chans), F32), V((crowd, chans), F32), V((crowd, chans), F32),
            V((nsh * crowd, chans), BF16), V((nsh * crowd, chans), BF16),
            V((crowd, chans), BF16), V((crowd, chans), BF16), V((crowd, inner), BF16),
            V((3, 3 * chans, chans), BF16), V((3, 3 * chans, chans), BF16),
            V((chans, chans), BF16), V((chans, 3 * chans), BF16), V((chans, chans), BF16),
            V((chans, 2 * inner), BF16), V((inner, chans), BF16),
            D((7,)), D((2,)), D((2 * STEPS, 2)), D((2 * STEPS, 2)),
            D((STEPS, subs, nsh)), D((STEPS, subs, nsh)), D((STEPS, subs, nsh)), D((STEPS, subs, nsh)),
            D((STEPS, subs)),
        ]
        result = pl.pallas_call(
            functools.partial(kernel, dims),
            out_shape=jax.ShapeDtypeStruct((tokens, chans), BF16),
            in_specs=[pl.BlockSpec(memory_space=pltpu.SMEM)] + [any_] * 8,
            out_specs=any_,
            scratch_shapes=scratch,
            compiler_params=pltpu.CompilerParams(
                collective_id=0, has_side_effects=True, vmem_limit_bytes=60 * 1024 * 1024
            ),
        )(
            timesteps,
            features.reshape(tokens, chans),
            conv_first.reshape(3, 3 * chans, chans),
            conv_second.reshape(3, 3 * chans, chans),
            time_weight[0], qkv_weight[0], attn_out[0], geglu_in[0], geglu_out[0],
        )
        return result.reshape(features.shape)

    return jax.shard_map(
        per_device,
        mesh=mesh,
        in_specs=(
            P(("groups", "section"), "shard", "halo", None, None),
            P(("groups", "section"), None),
            P("section", None, None, None, None),
            P("section", None, None, None, None),
            P("section", None, None),
            P("section", None, None),
            P("section", None, None),
            P("section", None, None),
            P("section", None, None),
        ),
        out_specs=P(("groups", "section"), "shard", "halo", None, None),
        check_vma=False,
    )
```

```python
import functools
import math

import jax
import jax.numpy as jnp
from jax import lax
from jax.experimental import pallas as pl
from jax.experimental.pallas import tpu as pltpu
from jax.sharding import PartitionSpec as P

HEAD_DIM = 64
GROUPS = 32
STEPS = 2
MESH = pl.DeviceIdType.MESH
F32 = jnp.float32
BF16 = jnp.bfloat16
BLK = 64
SUBS = 2
UNROLL = 4
SHIFTS = 4
PAD = 8


def matmul(a, b):
    return jnp.dot(a, b, preferred_element_type=F32)


def silu(u):
    return u * (1.0 / (1.0 + jnp.exp(-u)))


def kernel(dims, stamps, feat, cf_h, cs_h, tw_h, qkv_h, ao_h, gi_h, go_h, out, *scratch):
    (rows, width, chans, inner, nsh, nsec, subs) = dims
    (F, FX, first_rx, H, G, A, S, PB, O, stat_tx, stat_rx, edge_x, edge_h, emb, gmask, hmask, hmask_t,
     N, Q, K, V, PH, PL, OB, S2, ACT,
     cf, cs, tw, qkv, ao, gi, go,
     w_sem, x_send, x_recv, first_send, first_recv, halo_send, halo_recv, in_send, in_recv, out_send, out_recv, own_sem) = scratch
    tokens = rows * width
    part = tokens // nsh
    sub = part // subs
    crowd = nsh * sub
    rim = (rows + 2) * width
    me = lax.axis_index("shard")
    sec = lax.axis_index("section")
    side = lax.axis_index("halo")
    nxt = lax.rem(sec + 1, nsec)

    own = pltpu.make_async_copy(feat, FX, w_sem.at[7])
    own.start()
    loads = [
        pltpu.make_async_copy(src, dst, w_sem.at[i])
        for i, (src, dst) in enumerate(
            ((cf_h, cf), (cs_h, cs), (tw_h, tw), (qkv_h, qkv), (ao_h, ao), (gi_h, gi), (go_h, go))
        )
    ]
    for load in loads:
        load.start()

    def at(shard, section):
        return {"shard": shard, "section": section}

    barrier = pltpu.get_barrier_semaphore()
    peers = [{"halo": 1 - side}]
    for d in range(1, nsh):
        peers.append(at(lax.rem(me + d, nsh), sec))
    for e in sorted({1 % nsec, (nsec - 1) % nsec} - {0}):
        for d in range(nsh):
            peers.append(at(lax.rem(me + d, nsh), lax.rem(sec + e, nsec)))
        peers.append({"section": lax.rem(sec + e, nsec), "halo": 1 - side})
    for peer in peers:
        pl.semaphore_signal(barrier, inc=1, device_id=peer, device_id_type=MESH)
    pl.semaphore_wait(barrier, len(peers))

    edge_at = pl.multiple_of((1 - side) * (tokens - width), 16)
    piece = tokens // SHIFTS
    shifts = [
        pltpu.make_async_remote_copy(
            src_ref=feat.at[pl.ds(i * piece, piece)], dst_ref=F.at[0, pl.ds(i * piece, piece)],
            send_sem=x_send.at[i], recv_sem=x_recv.at[i],
            device_id={"section": nxt}, device_id_type=MESH,
        )
        for i in range(SHIFTS)
    ]
    firsts = [
        pltpu.make_async_remote_copy(
            src_ref=src, dst_ref=dst, send_sem=first_send.at[i], recv_sem=first_recv.at[i],
            device_id={"section": nxt, "halo": core}, device_id_type=MESH,
        )
        for i, (src, dst, core) in enumerate((
            (stat_tx.at[0], first_rx.at[0], side),
            (stat_tx.at[0], first_rx.at[1], 1 - side),
            (feat.at[pl.ds(edge_at, width)], edge_x.at[0], 1 - side),
        ))
    ]
    firsts[2].start()
    for i in range(SHIFTS // 2):
        shifts[i].start()
    stat_tx[...] = jnp.zeros_like(stat_tx)

    def fold(carry, v):
        s1, s2 = carry
        v = v.reshape(v.shape[0] // 8, 8, chans)
        return s1 + jnp.sum(v, axis=0), s2 + jnp.sum(v * v, axis=0)

    none = (jnp.zeros((8, chans), F32), jnp.zeros((8, chans), F32))

    def publish(slot, sums):
        stat_tx[slot, 0:1, :] = jnp.sum(sums[0], axis=0, keepdims=True)
        stat_tx[slot, 1:2, :] = jnp.sum(sums[1], axis=0, keepdims=True)

    own.wait()

    def own_total(i, carry):
        return fold(carry, FX[pl.ds(pl.multiple_of(i * BLK, BLK), BLK), :].astype(F32))
    publish(0, lax.fori_loop(0, tokens // BLK, own_total, none, unroll=UNROLL))
    firsts[0].start()
    firsts[1].start()
    for i in range(SHIFTS // 2, SHIFTS):
        shifts[i].start()

    per = chans // GROUPS
    ci = lax.broadcasted_iota(jnp.int32, (chans, chans), 0)
    cj = lax.broadcasted_iota(jnp.int32, (chans, chans), 1)
    gmask[...] = jnp.where(ci - lax.rem(ci, per) == cj - lax.rem(cj, per), 1.0, 0.0).astype(F32)
    lanes = hmask.shape[1]
    hi_ = lax.broadcasted_iota(jnp.int32, (chans, lanes), 0)
    hj_ = lax.broadcasted_iota(jnp.int32, (chans, lanes), 1)
    hmask[...] = jnp.where(hi_ - lax.rem(hi_, HEAD_DIM) == hj_ * HEAD_DIM, HEAD_DIM ** (-0.5), 0.0).astype(BF16)
    ti_ = lax.broadcasted_iota(jnp.int32, (lanes, chans), 0)
    tj_ = lax.broadcasted_iota(jnp.int32, (lanes, chans), 1)
    hmask_t[...] = jnp.where(tj_ - lax.rem(tj_, HEAD_DIM) == ti_ * HEAD_DIM, 1.0, 0.0).astype(BF16)
    zeros_rim = jnp.zeros((width, chans), F32)
    G[pl.ds(0, PAD), :] = jnp.zeros((PAD, chans), F32)
    G[pl.ds(PAD + rim, PAD), :] = jnp.zeros((PAD, chans), F32)
    G[pl.ds(PAD, width), :] = zeros_rim
    G[pl.ds(PAD + rim - width, width), :] = zeros_rim

    loads[2].wait()
    half = chans // 2
    lane = lax.broadcasted_iota(jnp.int32, (16, chans), 1)
    k_of = jnp.where(lane < half, lane, lane - half).astype(F32)
    frequency = jnp.exp(-math.log(10000.0) * k_of / half)
    for n in range(STEPS):
        angles = stamps[0, n].astype(F32) * frequency
        wave = jnp.where(lane < half, jnp.cos(angles), jnp.sin(angles))
        emb[n] = matmul(silu(wave).astype(BF16), tw[...])

    rim_at = pl.multiple_of(PAD + (1 - side) * (rim - width), 8)
    count = float(rows * 2 * width * per)

    def swap(slot, edge_src, edge_dst):
        copies = [
            pltpu.make_async_remote_copy(
                src_ref=src, dst_ref=dst, send_sem=halo_send.at[slot, i], recv_sem=halo_recv.at[slot, i],
                device_id={"halo": 1 - side}, device_id_type=MESH,
            )
            for i, (src, dst) in enumerate(
                ((edge_src, edge_dst), (stat_tx.at[slot], stat_rx.at[slot]))
            )
        ]
        return copies

    def moments(both):
        summed = jnp.dot(both, gmask[...], preferred_element_type=F32, precision=lax.Precision.HIGHEST)
        average = summed[0:1, :] / count
        second = summed[1:2, :] / count
        return average, lax.rsqrt(second - average * average + 1e-05)

    def activate(load, load_edge, both, arrivals=()):
        average, inverse = moments(both)

        def one(i, c):
            at_ = pl.multiple_of(i * BLK, BLK)
            G[pl.ds(PAD + width + at_, BLK), :] = silu((load(pl.ds(at_, BLK)) - average) * inverse)
            return c
        stages = max(len(arrivals), 1)
        for i in range(stages):
            if arrivals:
                arrivals[i].wait_recv()
            lax.fori_loop(i * (tokens // BLK) // stages, (i + 1) * (tokens // BLK) // stages, one, 0, unroll=2)
        G[pl.ds(rim_at, width), :] = silu((load_edge() - average) * inverse)
        col = lax.rem(lax.broadcasted_iota(jnp.int32, (width, chans), 0), width)

        def two(i, c):
            at_ = pl.multiple_of(i * width, width)
            window = G[pl.ds(at_, width + 2 * PAD), :]
            left = window[PAD - 1 : PAD - 1 + width]
            mid = window[PAD : PAD + width]
            right = window[PAD + 1 : PAD + 1 + width]
            dst = pl.ds(at_, width)
            A[dst, 0:chans] = jnp.where(col == 0, 0.0, left).astype(BF16)
            A[dst, chans : 2 * chans] = mid.astype(BF16)
            A[dst, 2 * chans :] = jnp.where(col == width - 1, 0.0, right).astype(BF16)
            return c
        lax.fori_loop(0, rows + 2, two, 0, unroll=5)

    def conv(weights, start, size):
        return sum(matmul(A[pl.ds(start + r * width, size), :], weights[r]) for r in range(3))

    def normalise(src):
        def one(i, c):
            at_ = pl.ds(pl.multiple_of(i * BLK, BLK), BLK)
            v = src(at_)
            centred = v - jnp.mean(v, axis=-1, keepdims=True)
            spread = jnp.mean(centred * centred, axis=-1, keepdims=True)
            N[at_, :] = (centred * lax.rsqrt(spread + 1e-05)).astype(BF16)
            return c
        lax.fori_loop(0, crowd // BLK, one, 0, unroll=UNROLL)

    def gather_copy(n, k, d):
        to = lax.rem(me + d, nsh)
        return pltpu.make_async_remote_copy(
            src_ref=S.at[n, k, to], dst_ref=PB.at[n, k, me],
            send_sem=in_send.at[n, k, d], recv_sem=in_recv.at[n, k, d],
            device_id={"shard": to}, device_id_type=MESH,
        )

    def return_copy(n, k, d):
        last = n == STEPS - 1
        target = out if last else F.at[n + 1]
        landing = target.at[pl.ds(pl.multiple_of(me * part + k * sub, 16), sub)]
        to = lax.rem(me + d, nsh)
        if d == 0 and (last or nsec == 1):
            return pltpu.make_async_copy(O.at[n, k, me], landing, own_sem.at[n, k])
        return pltpu.make_async_remote_copy(
            src_ref=O.at[n, k, to], dst_ref=landing,
            send_sem=out_send.at[n, k, d], recv_sem=out_recv.at[n, k, d],
            device_id=at(to, sec if last else nxt), device_id_type=MESH,
        )

    def pixels(n, k):
        stream = PB.at[n, k]

        def load_p(s):
            return stream.reshape(crowd, chans)[s, :].astype(F32)
        normalise(load_p)
        proj = matmul(N[...], qkv[...]).astype(BF16)
        Q[...] = proj[:, :chans].astype(F32)
        K[...] = proj[:, chans : 2 * chans].astype(F32)
        V[...] = proj[:, 2 * chans :].astype(F32)

        def frame(f, c):
            q = Q[pl.ds(pl.multiple_of(f * sub, 16), sub), :]
            start = pl.multiple_of(f * crowd, 16)
            for g in range(nsh):
                prod = q * K[g * sub : (g + 1) * sub, :]
                high = prod.astype(BF16)
                PH[pl.ds(start + g * sub, sub), :] = high
                PL[pl.ds(start + g * sub, sub), :] = (prod - high.astype(F32)).astype(BF16)
            score = matmul(PH[pl.ds(start, crowd), :], hmask[...]) + matmul(PL[pl.ds(start, crowd), :], hmask[...])
            pieces = [score[g * sub : (g + 1) * sub] for g in range(nsh)]
            top = functools.reduce(jnp.maximum, pieces)
            pieces = [jnp.exp(p - top) for p in pieces]
            scale = 1.0 / functools.reduce(jnp.add, pieces)
            weights = jnp.concatenate([(p * scale).astype(BF16) for p in pieces], axis=0)
            weights = matmul(weights, hmask_t[...])
            mixed = weights[0:sub] * V[0:sub, :]
            for g in range(1, nsh):
                mixed = mixed + weights[g * sub : (g + 1) * sub] * V[g * sub : (g + 1) * sub, :]
            OB[pl.ds(pl.multiple_of(f * sub, 16), sub), :] = mixed.astype(BF16)
            return c
        lax.fori_loop(0, nsh, frame, 0, unroll=4)

        S2[...] = (matmul(OB[...], ao[...]) + stream[...].reshape(crowd, chans).astype(F32)).astype(BF16)
        normalise(lambda s: S2[s, :].astype(F32))
        wide = 256
        for j in range(inner // wide):
            value = matmul(N[...], gi[:, j * wide : (j + 1) * wide])
            gate = matmul(N[...], gi[:, inner + j * wide : inner + (j + 1) * wide])
            gelu = 0.5 * gate * (1.0 + lax.erf(gate * (0.5 ** 0.5)))
            ACT[:, j * wide : (j + 1) * wide] = (value * gelu).astype(BF16)
        O[n, k] = (matmul(ACT[...], go[...]) + S2[...].astype(F32)).astype(BF16).reshape(nsh, sub, chans)

    for n in range(STEPS):
        field = F.at[n]

        def load_x(s, field=field):
            return field[s, :].astype(F32)

        if n == 0:
            for c in firsts:
                c.wait()
            activate(load_x, lambda: edge_x[0].astype(F32), first_rx[0] + first_rx[1], shifts)
            for c in shifts:
                c.wait_send()
            loads[0].wait()
        else:
            swaps = swap(2 * n, field.at[pl.ds(edge_at, width)], edge_x.at[n])
            swaps[0].start()
            publish(2 * n, sums)
            swaps[1].start()
            for c in swaps:
                c.wait()
            activate(load_x, lambda n=n: edge_x[n].astype(F32), stat_tx[2 * n] + stat_rx[2 * n])
        sums = none
        for i in range(2):
            rows_ = pl.ds(i * (tokens // 2), tokens // 2)
            h1 = conv(cf, i * (tokens // 2), tokens // 2) + emb[n, 0:1, :]
            H[n, rows_, :] = h1
            sums = fold(sums, h1)

        slot = 2 * n + 1
        swaps = swap(slot, H.at[n, pl.ds(edge_at, width)], edge_h.at[n])
        swaps[0].start()
        publish(slot, sums)
        swaps[1].start()
        for c in swaps:
            c.wait()
        activate(lambda s, n=n: H[n, s, :], lambda n=n: edge_h[n], stat_tx[slot] + stat_rx[slot])
        if n == 0:
            loads[1].wait()
        for k in range(subs):
            spans = [j * part + k * sub for j in range(nsh)]
            total = sum(
                matmul(jnp.concatenate([A[pl.ds(r * width + a, sub), :] for a in spans], axis=0), cs[r])
                for r in range(3)
            )
            base = jnp.concatenate([field[pl.ds(a, sub), :] for a in spans], axis=0)
            S[n, k] = (total + base.astype(F32)).astype(BF16).reshape(nsh, sub, chans)
            for d in range(1, nsh):
                gather_copy(n, k, d).start()
            PB[n, k, me] = S[n, k, me]

        if n == 0:
            for i in (3, 4, 5, 6):
                loads[i].wait()

        def temporal(k, carry, n=n):
            for d in range(1, nsh):
                gather_copy(n, k, d).wait_recv()
            pixels(n, k)
            for d in range(nsh):
                return_copy(n, k, d).start()
            return carry
        lax.fori_loop(0, subs, temporal, 0)

        sums = none
        for k in range(subs):
            for d in range(nsh):
                return_copy(n, k, d).wait()
            if n < STEPS - 1:
                for j in range(nsh):
                    sums = fold(sums, F[n + 1, pl.ds(j * part + k * sub, sub), :].astype(F32))
        for k in range(subs):
            for d in range(1, nsh):
                gather_copy(n, k, d).wait_send()


def solution(mesh):
    nsh, nsec = mesh.shape["shard"], mesh.shape["section"]

    def per_device(features, timesteps, conv_first, conv_second, time_weight, qkv_weight,
                   attn_out, geglu_in, geglu_out):
        _, _, rows, width, chans = features.shape
        inner = geglu_out.shape[1]
        tokens = rows * width
        part = tokens // nsh
        rim = (rows + 2) * width
        subs = min(SUBS, part // 16)
        dims = (rows, width, chans, inner, nsh, nsec, subs)
        sub = part // subs
        crowd = nsh * sub
        any_ = pl.BlockSpec(memory_space=pl.ANY)
        V = pltpu.VMEM
        D = pltpu.SemaphoreType.DMA
        scratch = [
            V((STEPS, tokens, chans), BF16),
            V((tokens, chans), BF16),
            V((2, 8, chans), F32),
            V((STEPS, tokens, chans), F32),
            V((rim + 2 * PAD, chans), F32),
            V((rim, 3 * chans), BF16),
            V((STEPS, subs, nsh, sub, chans), BF16),
            V((STEPS, subs, nsh, sub, chans), BF16),
            V((STEPS, subs, nsh, sub, chans), BF16),
            V((2 * STEPS, 8, chans), F32),
            V((2 * STEPS, 8, chans), F32),
            V((STEPS, width, chans), BF16),
            V((STEPS, width, chans), F32),
            V((STEPS, 16, chans), F32),
            V((chans, chans), F32),
            V((chans, 128), BF16),
            V((128, chans), BF16),
            V((crowd, chans), BF16),
            V((crowd, chans), F32), V((crowd, chans), F32), V((crowd, chans), F32),
            V((nsh * crowd, chans), BF16), V((nsh * crowd, chans), BF16),
            V((crowd, chans), BF16), V((crowd, chans), BF16), V((crowd, inner), BF16),
            V((3, 3 * chans, chans), BF16), V((3, 3 * chans, chans), BF16),
            V((chans, chans), BF16), V((chans, 3 * chans), BF16), V((chans, chans), BF16),
            V((chans, 2 * inner), BF16), V((inner, chans), BF16),
            D((8,)), D((SHIFTS,)), D((SHIFTS,)), D((3,)), D((3,)), D((2 * STEPS, 2)), D((2 * STEPS, 2)),
            D((STEPS, subs, nsh)), D((STEPS, subs, nsh)), D((STEPS, subs, nsh)), D((STEPS, subs, nsh)),
            D((STEPS, subs)),
        ]
        result = pl.pallas_call(
            functools.partial(kernel, dims),
            out_shape=jax.ShapeDtypeStruct((tokens, chans), BF16),
            in_specs=[pl.BlockSpec(memory_space=pltpu.SMEM)] + [any_] * 8,
            out_specs=any_,
            scratch_shapes=scratch,
            compiler_params=pltpu.CompilerParams(
                collective_id=0, has_side_effects=True, vmem_limit_bytes=60 * 1024 * 1024
            ),
        )(
            timesteps,
            features.reshape(tokens, chans),
            conv_first.reshape(3, 3 * chans, chans),
            conv_second.reshape(3, 3 * chans, chans),
            time_weight[0], qkv_weight[0], attn_out[0], geglu_in[0], geglu_out[0],
        )
        return result.reshape(features.shape)

    return jax.shard_map(
        per_device,
        mesh=mesh,
        in_specs=(
            P(("groups", "section"), "shard", "halo", None, None),
            P(("groups", "section"), None),
            P("section", None, None, None, None),
            P("section", None, None, None, None),
            P("section", None, None),
            P("section", None, None),
            P("section", None, None),
            P("section", None, None),
            P("section", None, None),
        ),
        out_specs=P(("groups", "section"), "shard", "halo", None, None),
        check_vma=False,
    )
```

```python
import functools
import math

import jax
import jax.numpy as jnp
from jax import lax
from jax.experimental import pallas as pl
from jax.experimental.pallas import tpu as pltpu
from jax.sharding import PartitionSpec as P

HEAD_DIM = 64
GROUPS = 32
STEPS = 2
MESH = pl.DeviceIdType.MESH
F32 = jnp.float32
BF16 = jnp.bfloat16
BLK = 64
SUBS = 2
UNROLL = 4
SHIFTS = 4
PAD = 8


def matmul(a, b):
    return jnp.dot(a, b, preferred_element_type=F32)


def matmul_t(a, b):
    return lax.dot_general(a, b, (((1,), (1,)), ((), ())), preferred_element_type=F32)


def silu(u):
    return u * (1.0 / (1.0 + jnp.exp(-u)))


def kernel(dims, stamps, feat, cf_h, cs_h, tw_h, qkv_h, ao_h, gi_h, go_h, out, *scratch):
    (rows, width, chans, inner, nsh, nsec, subs) = dims
    (F, FX, first_rx, H, G, A, S, PB, O, stat_tx, stat_rx, edge_x, edge_h, emb, gmask, hmask, hmask_t,
     N, Q, K, V, PH, PL, OB, S2, ACT,
     cf, cs, tw, qkv, ao, gi, go,
     w_sem, x_send, x_recv, first_send, first_recv, halo_send, halo_recv, in_send, in_recv, out_send, out_recv, own_sem) = scratch
    tokens = rows * width
    part = tokens // nsh
    sub = part // subs
    crowd = nsh * sub
    rim = (rows + 2) * width
    me = lax.axis_index("shard")
    sec = lax.axis_index("section")
    side = lax.axis_index("halo")
    nxt = lax.rem(sec + 1, nsec)

    own = pltpu.make_async_copy(feat, FX, w_sem.at[7])
    own.start()
    loads = [
        pltpu.make_async_copy(src, dst, w_sem.at[i])
        for i, (src, dst) in enumerate(
            ((cf_h, cf), (cs_h, cs), (tw_h, tw), (qkv_h, qkv), (ao_h, ao), (gi_h, gi), (go_h, go))
        )
    ]
    for load in loads:
        load.start()

    def at(shard, section):
        return {"shard": shard, "section": section}

    barrier = pltpu.get_barrier_semaphore()
    peers = [{"halo": 1 - side}]
    for d in range(1, nsh):
        peers.append(at(lax.rem(me + d, nsh), sec))
    for e in sorted({1 % nsec, (nsec - 1) % nsec} - {0}):
        for d in range(nsh):
            peers.append(at(lax.rem(me + d, nsh), lax.rem(sec + e, nsec)))
        peers.append({"section": lax.rem(sec + e, nsec), "halo": 1 - side})
    for peer in peers:
        pl.semaphore_signal(barrier, inc=1, device_id=peer, device_id_type=MESH)
    pl.semaphore_wait(barrier, len(peers))

    edge_at = pl.multiple_of((1 - side) * (tokens - width), 16)
    piece = tokens // SHIFTS
    shifts = [
        pltpu.make_async_remote_copy(
            src_ref=feat.at[pl.ds(i * piece, piece)], dst_ref=F.at[0, pl.ds(i * piece, piece)],
            send_sem=x_send.at[i], recv_sem=x_recv.at[i],
            device_id={"section": nxt}, device_id_type=MESH,
        )
        for i in range(SHIFTS)
    ]
    firsts = [
        pltpu.make_async_remote_copy(
            src_ref=src, dst_ref=dst, send_sem=first_send.at[i], recv_sem=first_recv.at[i],
            device_id={"section": nxt, "halo": core}, device_id_type=MESH,
        )
        for i, (src, dst, core) in enumerate((
            (stat_tx.at[0], first_rx.at[0], side),
            (stat_tx.at[0], first_rx.at[1], 1 - side),
            (feat.at[pl.ds(edge_at, width)], edge_x.at[0], 1 - side),
        ))
    ]
    firsts[2].start()
    for i in range(SHIFTS // 2):
        shifts[i].start()
    stat_tx[...] = jnp.zeros_like(stat_tx)

    def fold(carry, v):
        s1, s2 = carry
        v = v.reshape(v.shape[0] // 8, 8, chans)
        return s1 + jnp.sum(v, axis=0), s2 + jnp.sum(v * v, axis=0)

    none = (jnp.zeros((8, chans), F32), jnp.zeros((8, chans), F32))

    def publish(slot, sums):
        stat_tx[slot, 0:1, :] = jnp.sum(sums[0], axis=0, keepdims=True)
        stat_tx[slot, 1:2, :] = jnp.sum(sums[1], axis=0, keepdims=True)

    own.wait()

    def own_total(i, carry):
        return fold(carry, FX[pl.ds(pl.multiple_of(i * BLK, BLK), BLK), :].astype(F32))
    publish(0, lax.fori_loop(0, tokens // BLK, own_total, none, unroll=UNROLL))
    firsts[0].start()
    firsts[1].start()
    for i in range(SHIFTS // 2, SHIFTS):
        shifts[i].start()

    per = chans // GROUPS
    ci = lax.broadcasted_iota(jnp.int32, (chans, chans), 0)
    cj = lax.broadcasted_iota(jnp.int32, (chans, chans), 1)
    gmask[...] = jnp.where(ci - lax.rem(ci, per) == cj - lax.rem(cj, per), 1.0, 0.0).astype(F32)
    lanes = hmask.shape[1]
    hi_ = lax.broadcasted_iota(jnp.int32, (chans, lanes), 0)
    hj_ = lax.broadcasted_iota(jnp.int32, (chans, lanes), 1)
    hmask[...] = jnp.where(hi_ - lax.rem(hi_, HEAD_DIM) == hj_ * HEAD_DIM, HEAD_DIM ** (-0.5), 0.0).astype(BF16)
    ti_ = lax.broadcasted_iota(jnp.int32, (lanes, chans), 0)
    tj_ = lax.broadcasted_iota(jnp.int32, (lanes, chans), 1)
    hmask_t[...] = jnp.where(tj_ - lax.rem(tj_, HEAD_DIM) == ti_ * HEAD_DIM, 1.0, 0.0).astype(BF16)
    zeros_rim = jnp.zeros((width, chans), F32)
    G[pl.ds(0, PAD), :] = jnp.zeros((PAD, chans), F32)
    G[pl.ds(PAD + rim, PAD), :] = jnp.zeros((PAD, chans), F32)
    G[pl.ds(PAD, width), :] = zeros_rim
    G[pl.ds(PAD + rim - width, width), :] = zeros_rim

    loads[2].wait()
    half = chans // 2
    lane = lax.broadcasted_iota(jnp.int32, (16, chans), 1)
    k_of = jnp.where(lane < half, lane, lane - half).astype(F32)
    frequency = jnp.exp(-math.log(10000.0) * k_of / half)
    for n in range(STEPS):
        angles = stamps[0, n].astype(F32) * frequency
        wave = jnp.where(lane < half, jnp.cos(angles), jnp.sin(angles))
        emb[n] = matmul(silu(wave).astype(BF16), tw[...])

    rim_at = pl.multiple_of(PAD + (1 - side) * (rim - width), 8)
    count = float(rows * 2 * width * per)

    def swap(slot, edge_src, edge_dst):
        copies = [
            pltpu.make_async_remote_copy(
                src_ref=src, dst_ref=dst, send_sem=halo_send.at[slot, i], recv_sem=halo_recv.at[slot, i],
                device_id={"halo": 1 - side}, device_id_type=MESH,
            )
            for i, (src, dst) in enumerate(
                ((edge_src, edge_dst), (stat_tx.at[slot], stat_rx.at[slot]))
            )
        ]
        return copies

    def moments(both):
        summed = jnp.dot(both, gmask[...], preferred_element_type=F32, precision=lax.Precision.HIGHEST)
        average = summed[0:1, :] / count
        second = summed[1:2, :] / count
        return average, lax.rsqrt(second - average * average + 1e-05)

    def activate(load, load_edge, both, arrivals=()):
        average, inverse = moments(both)

        def one(i, c):
            at_ = pl.multiple_of(i * BLK, BLK)
            G[pl.ds(PAD + width + at_, BLK), :] = silu((load(pl.ds(at_, BLK)) - average) * inverse)
            return c
        stages = max(len(arrivals), 1)
        for i in range(stages):
            if arrivals:
                arrivals[i].wait_recv()
            lax.fori_loop(i * (tokens // BLK) // stages, (i + 1) * (tokens // BLK) // stages, one, 0, unroll=2)
        G[pl.ds(rim_at, width), :] = silu((load_edge() - average) * inverse)
        col = lax.rem(lax.broadcasted_iota(jnp.int32, (width, chans), 0), width)

        def two(i, c):
            at_ = pl.multiple_of(i * width, width)
            window = G[pl.ds(at_, width + 2 * PAD), :]
            left = window[PAD - 1 : PAD - 1 + width]
            mid = window[PAD : PAD + width]
            right = window[PAD + 1 : PAD + 1 + width]
            dst = pl.ds(at_, width)
            A[dst, 0:chans] = jnp.where(col == 0, 0.0, left).astype(BF16)
            A[dst, chans : 2 * chans] = mid.astype(BF16)
            A[dst, 2 * chans :] = jnp.where(col == width - 1, 0.0, right).astype(BF16)
            return c
        lax.fori_loop(0, rows + 2, two, 0, unroll=5)

    def conv(weights, start, size):
        return sum(matmul(A[pl.ds(start + r * width, size), :], weights[r]) for r in range(3))

    def normalise(src):
        def one(i, c):
            at_ = pl.ds(pl.multiple_of(i * BLK, BLK), BLK)
            v = src(at_)
            centred = v - jnp.mean(v, axis=-1, keepdims=True)
            spread = jnp.mean(centred * centred, axis=-1, keepdims=True)
            N[at_, :] = (centred * lax.rsqrt(spread + 1e-05)).astype(BF16)
            return c
        lax.fori_loop(0, crowd // BLK, one, 0, unroll=UNROLL)

    def gather_copy(n, k, d):
        to = lax.rem(me + d, nsh)
        return pltpu.make_async_remote_copy(
            src_ref=S.at[n, k, to], dst_ref=PB.at[n, k, me],
            send_sem=in_send.at[n, k, d], recv_sem=in_recv.at[n, k, d],
            device_id={"shard": to}, device_id_type=MESH,
        )

    def return_copy(n, k, d):
        last = n == STEPS - 1
        target = out if last else F.at[n + 1]
        landing = target.at[pl.ds(pl.multiple_of(me * part + k * sub, 16), sub)]
        to = lax.rem(me + d, nsh)
        if d == 0 and (last or nsec == 1):
            return pltpu.make_async_copy(O.at[n, k, me], landing, own_sem.at[n, k])
        return pltpu.make_async_remote_copy(
            src_ref=O.at[n, k, to], dst_ref=landing,
            send_sem=out_send.at[n, k, d], recv_sem=out_recv.at[n, k, d],
            device_id=at(to, sec if last else nxt), device_id_type=MESH,
        )

    def pixels(n, k):
        stream = PB.at[n, k]

        def load_p(s):
            return stream.reshape(crowd, chans)[s, :].astype(F32)
        normalise(load_p)
        proj = matmul(N[...], qkv[...]).astype(BF16)
        Q[...] = proj[:, :chans].astype(F32)
        K[...] = proj[:, chans : 2 * chans].astype(F32)
        V[...] = proj[:, 2 * chans :].astype(F32)

        def frame(f, c):
            q = Q[pl.ds(pl.multiple_of(f * sub, 16), sub), :]
            start = pl.multiple_of(f * crowd, 16)
            for g in range(nsh):
                prod = q * K[g * sub : (g + 1) * sub, :]
                high = prod.astype(BF16)
                PH[pl.ds(start + g * sub, sub), :] = high
                PL[pl.ds(start + g * sub, sub), :] = (prod - high.astype(F32)).astype(BF16)
            score = matmul(PH[pl.ds(start, crowd), :], hmask[...]) + matmul(PL[pl.ds(start, crowd), :], hmask[...])
            pieces = [score[g * sub : (g + 1) * sub] for g in range(nsh)]
            top = functools.reduce(jnp.maximum, pieces)
            pieces = [jnp.exp(p - top) for p in pieces]
            scale = 1.0 / functools.reduce(jnp.add, pieces)
            weights = jnp.concatenate([(p * scale).astype(BF16) for p in pieces], axis=0)
            weights = matmul(weights, hmask_t[...])
            mixed = weights[0:sub] * V[0:sub, :]
            for g in range(1, nsh):
                mixed = mixed + weights[g * sub : (g + 1) * sub] * V[g * sub : (g + 1) * sub, :]
            OB[pl.ds(pl.multiple_of(f * sub, 16), sub), :] = mixed.astype(BF16)
            return c
        lax.fori_loop(0, nsh, frame, 0, unroll=4)

        S2[...] = (matmul(OB[...], ao[...]) + stream[...].reshape(crowd, chans).astype(F32)).astype(BF16)
        normalise(lambda s: S2[s, :].astype(F32))
        wide = 256
        for j in range(inner // wide):
            value = matmul(N[...], gi[:, j * wide : (j + 1) * wide])
            gate = matmul(N[...], gi[:, inner + j * wide : inner + (j + 1) * wide])
            gelu = 0.5 * gate * (1.0 + lax.erf(gate * (0.5 ** 0.5)))
            ACT[:, j * wide : (j + 1) * wide] = (value * gelu).astype(BF16)
        O[n, k] = (matmul_t(ACT[...], go[...]) + S2[...].astype(F32)).astype(BF16).reshape(nsh, sub, chans)

    for n in range(STEPS):
        field = F.at[n]

        def load_x(s, field=field):
            return field[s, :].astype(F32)

        if n == 0:
            for c in firsts:
                c.wait()
            activate(load_x, lambda: edge_x[0].astype(F32), first_rx[0] + first_rx[1], shifts)
            for c in shifts:
                c.wait_send()
            loads[0].wait()
        else:
            swaps = swap(2 * n, field.at[pl.ds(edge_at, width)], edge_x.at[n])
            swaps[0].start()
            publish(2 * n, sums)
            swaps[1].start()
            for c in swaps:
                c.wait()
            activate(load_x, lambda n=n: edge_x[n].astype(F32), stat_tx[2 * n] + stat_rx[2 * n])
        sums = none
        for i in range(2):
            rows_ = pl.ds(i * (tokens // 2), tokens // 2)
            h1 = conv(cf, i * (tokens // 2), tokens // 2) + emb[n, 0:1, :]
            H[n, rows_, :] = h1
            sums = fold(sums, h1)

        slot = 2 * n + 1
        swaps = swap(slot, H.at[n, pl.ds(edge_at, width)], edge_h.at[n])
        swaps[0].start()
        publish(slot, sums)
        swaps[1].start()
        for c in swaps:
            c.wait()
        activate(lambda s, n=n: H[n, s, :], lambda n=n: edge_h[n], stat_tx[slot] + stat_rx[slot])
        if n == 0:
            loads[1].wait()
        for k in range(subs):
            spans = [j * part + k * sub for j in range(nsh)]
            total = sum(
                matmul(jnp.concatenate([A[pl.ds(r * width + a, sub), :] for a in spans], axis=0), cs[r])
                for r in range(3)
            )
            base = jnp.concatenate([field[pl.ds(a, sub), :] for a in spans], axis=0)
            S[n, k] = (total + base.astype(F32)).astype(BF16).reshape(nsh, sub, chans)
            for d in range(1, nsh):
                gather_copy(n, k, d).start()
            PB[n, k, me] = S[n, k, me]

        if n == 0:
            for i in (3, 4, 5, 6):
                loads[i].wait()

        def temporal(k, carry, n=n):
            for d in range(1, nsh):
                gather_copy(n, k, d).wait_recv()
            pixels(n, k)
            for d in range(nsh):
                return_copy(n, k, d).start()
            return carry
        lax.fori_loop(0, subs, temporal, 0)

        sums = none
        for k in range(subs):
            for d in range(nsh):
                return_copy(n, k, d).wait()
            if n < STEPS - 1:
                for j in range(nsh):
                    sums = fold(sums, F[n + 1, pl.ds(j * part + k * sub, sub), :].astype(F32))
        for k in range(subs):
            for d in range(1, nsh):
                gather_copy(n, k, d).wait_send()


def solution(mesh):
    nsh, nsec = mesh.shape["shard"], mesh.shape["section"]

    def per_device(features, timesteps, conv_first, conv_second, time_weight, qkv_weight,
                   attn_out, geglu_in, geglu_out):
        _, _, rows, width, chans = features.shape
        inner = geglu_out.shape[1]
        tokens = rows * width
        part = tokens // nsh
        rim = (rows + 2) * width
        subs = min(SUBS, part // 16)
        dims = (rows, width, chans, inner, nsh, nsec, subs)
        sub = part // subs
        crowd = nsh * sub
        any_ = pl.BlockSpec(memory_space=pl.ANY)
        V = pltpu.VMEM
        D = pltpu.SemaphoreType.DMA
        scratch = [
            V((STEPS, tokens, chans), BF16),
            V((tokens, chans), BF16),
            V((2, 8, chans), F32),
            V((STEPS, tokens, chans), F32),
            V((rim + 2 * PAD, chans), F32),
            V((rim, 3 * chans), BF16),
            V((STEPS, subs, nsh, sub, chans), BF16),
            V((STEPS, subs, nsh, sub, chans), BF16),
            V((STEPS, subs, nsh, sub, chans), BF16),
            V((2 * STEPS, 8, chans), F32),
            V((2 * STEPS, 8, chans), F32),
            V((STEPS, width, chans), BF16),
            V((STEPS, width, chans), F32),
            V((STEPS, 16, chans), F32),
            V((chans, chans), F32),
            V((chans, 128), BF16),
            V((128, chans), BF16),
            V((crowd, chans), BF16),
            V((crowd, chans), F32), V((crowd, chans), F32), V((crowd, chans), F32),
            V((nsh * crowd, chans), BF16), V((nsh * crowd, chans), BF16),
            V((crowd, chans), BF16), V((crowd, chans), BF16), V((crowd, inner), BF16),
            V((3, 3 * chans, chans), BF16), V((3, 3 * chans, chans), BF16),
            V((chans, chans), BF16), V((chans, 3 * chans), BF16), V((chans, chans), BF16),
            V((chans, 2 * inner), BF16), V((chans, inner), BF16),
            D((8,)), D((SHIFTS,)), D((SHIFTS,)), D((3,)), D((3,)), D((2 * STEPS, 2)), D((2 * STEPS, 2)),
            D((STEPS, subs, nsh)), D((STEPS, subs, nsh)), D((STEPS, subs, nsh)), D((STEPS, subs, nsh)),
            D((STEPS, subs)),
        ]
        result = pl.pallas_call(
            functools.partial(kernel, dims),
            out_shape=jax.ShapeDtypeStruct((tokens, chans), BF16),
            in_specs=[pl.BlockSpec(memory_space=pltpu.SMEM)] + [any_] * 8,
            out_specs=any_,
            scratch_shapes=scratch,
            compiler_params=pltpu.CompilerParams(
                collective_id=0, has_side_effects=True, vmem_limit_bytes=60 * 1024 * 1024
            ),
        )(
            timesteps,
            features.reshape(tokens, chans),
            conv_first.reshape(3, 3 * chans, chans),
            conv_second.reshape(3, 3 * chans, chans),
            time_weight[0], qkv_weight[0], attn_out[0], geglu_in[0], jnp.swapaxes(geglu_out[0], 0, 1),
        )
        return result.reshape(features.shape)

    return jax.shard_map(
        per_device,
        mesh=mesh,
        in_specs=(
            P(("groups", "section"), "shard", "halo", None, None),
            P(("groups", "section"), None),
            P("section", None, None, None, None),
            P("section", None, None, None, None),
            P("section", None, None),
            P("section", None, None),
            P("section", None, None),
            P("section", None, None),
            P("section", None, None),
        ),
        out_specs=P(("groups", "section"), "shard", "halo", None, None),
        check_vma=False,
    )
```
